32 devices in a mesh: ell: 16 (over z, y, core), chan: 2 (over x).
Axes of the slice: x: 2, y: 2, z: 4, core: 2. Of those that a mesh axis runs over, the one named last changes fastest.
Arguments:
- sky_alm: bfloat16 [4, 1024, 24576], P('chan', 'ell'), may hold values from -6 to 6
- beam_transfer: bfloat16 [4, 16, 128, 16, 1536], P('chan', 'ell'), may hold values from -0.15625 to 0.15625
- slot_rows: int32 [16, 128], P('ell'), may hold values from 0 to 127, as said below
- block_count: int32 [16], P('ell'), may hold values from 1 to 128, as said below
Outputs:
- visibility: bfloat16 [4, 128, 16, 1024], P('chan', 'ell')
The draws below stay inside these ranges and needn't reach their ends.
Inputs may be any that keep to these rules, and one draw needn't show every extreme that they name: `block_count`: every l-block has at least one live slot, and some l-block has exactly 128. `slot_rows`: the 128 entries of one l-block are distinct baselines; only the first block_count of them are live.
All inputs are finite; a program needn't handle non-finite values.
Results may differ from the reference program's by a relative error of at most 0.012.
Values may be sent and summed in bfloat16 or wider, within the bound.
A program may use at most 192 MiB of HBM per device.

```python
import jax
import jax.numpy as jnp
from jax import lax

VC = 16
R = 1024
CAP = 128
NCH = 4
LS = 24576
NBLK = 16
KB = 1536
NB = 128


def draw_block_count(key, part):
    first_key, second_key, third_key = jax.random.split(key, 3)
    wide_draw = jax.random.randint(first_key, (NBLK,), 1, CAP + 1)
    narrow_draw = jax.random.randint(second_key, (NBLK,), max(1, CAP // 4), CAP + 1)
    counts = jnp.minimum(wide_draw, narrow_draw)
    busiest = jax.random.randint(third_key, (), 0, NBLK)
    return jnp.where(jnp.arange(NBLK) == busiest, CAP, counts).astype(jnp.int32)


def draw_slot_rows(key, part):
    block_keys = jax.random.split(key, NBLK)

    def pick_rows(one_key):
        return jax.random.permutation(one_key, NB)[:CAP]
    return jax.vmap(pick_rows)(block_keys).astype(jnp.int32)


def shard_levels(key, extent, cuts, low, top_value):
    loudness = 1.0
    for axis_at, parts in cuts:
        heights = jax.random.uniform(jax.random.fold_in(jax.random.fold_in(key, 6), axis_at), (parts,), jnp.float32, low / len(cuts), top_value / len(cuts))
        loudness = loudness * jnp.repeat(jnp.exp(heights), extent[axis_at] // parts).reshape((-1,) + (1,) * (len(extent) - 1 - axis_at))
    return loudness


def noise(rng, extent, deviation, most, shards=(), kind=jnp.bfloat16):
    drawn = jax.random.normal(rng, extent, jnp.float32) * deviation
    if len(shards) > 0:
        drawn = shard_levels(rng, extent, shards, -0.22, 0.18) * drawn
    return jnp.clip(drawn, min=-most, max=most).astype(kind)


def setup_inputs(seed: int = 0) -> dict:
    key_list = jax.random.split(jax.random.key(seed), 5)
    sky_alm = noise(key_list[0], (NCH, R, LS), 1.0, 6.0, ((0, 2), (1, 16)))
    beam_transfer = noise(key_list[1], (NCH, NBLK, CAP, VC, KB), KB ** -0.5, 0.15625, ((0, 2), (1, 16)))
    slot_rows = draw_slot_rows(jax.random.fold_in(key_list[4], 71), 0)
    block_count = draw_block_count(jax.random.fold_in(key_list[4], 71), 0)
    return {"sky_alm": sky_alm, "beam_transfer": beam_transfer, "slot_rows": slot_rows, "block_count": block_count}


def reference(sky_alm, beam_transfer, slot_rows, block_count):
    channels = sky_alm.shape[0]
    slot_number = jnp.arange(CAP, dtype=jnp.int32)

    def one_block(running, block_index):
        block_beam = lax.dynamic_index_in_dim(beam_transfer, block_index, 1, keepdims=False)
        block_sky = lax.dynamic_slice_in_dim(sky_alm, block_index * KB, KB, 2)
        partial_sum = jnp.einsum("cpvk,crk->cpvr", block_beam.astype(jnp.float32), block_sky.astype(jnp.float32))
        live_count = lax.dynamic_index_in_dim(block_count, block_index, 0, keepdims=False)
        inside = slot_number < live_count
        partial_sum = jnp.where(inside[None, :, None, None], partial_sum, jnp.zeros_like(partial_sum))
        rounded = lax.optimization_barrier(partial_sum.astype(jnp.bfloat16))
        rows_here = lax.dynamic_index_in_dim(slot_rows, block_index, 0, keepdims=False)
        running = running.at[:, rows_here].add(rounded.astype(jnp.float32))
        return running, None

    start_value = jnp.zeros((channels, NB, VC, R), jnp.float32)
    total, unused = lax.scan(one_block, start_value, jnp.arange(NBLK, dtype=jnp.int32))
    return total.astype(jnp.bfloat16)
```

```python
import functools

import jax
import jax.numpy as jnp
from jax import lax
from jax.experimental import pallas as pl
from jax.experimental.pallas import tpu as pltpu
from jax.sharding import PartitionSpec as P

BL_OWN = 8
LOOKAHEAD = 2
STEP_ROWS = 16
GROUP = 4


def bit(value, at):
    return (value // (1 << at)) % 2


def kernel(n, levels, quarters, slot_ref, sky_ref, beam_ref, out_ref, beam_in, dense, held, part, got, place,
           beam_sem, own_sem, sky_send, sky_recv, sum_send, sum_recv):
    me = lax.axis_index("ell")
    channels, capacity, components = beam_in.shape[0], beam_in.shape[1] - 1, beam_in.shape[2]
    depth = beam_in.shape[3]
    phases = channels * quarters
    rows = STEP_ROWS
    width = n * rows

    def dest_of(position):
        total = 0
        for level in range(levels):
            flip = bit(position, levels - 1 - level)
            total = total + ((bit(me, level) + flip) % 2) * (1 << level)
        return total

    def partner_of(level):
        return me + (1 - 2 * bit(me, level)) * (1 << level)

    def sky_block(phase, owner):
        channel, quarter = phase // quarters, phase % quarters
        return sky_ref.at[
            channel,
            pl.ds(pl.multiple_of(quarter * rows, rows), rows),
            pl.ds(pl.multiple_of(owner * depth, 128), depth),
        ]

    def send_sky(phase):
        pltpu.make_async_copy(sky_block(phase, me), held.at[phase, me], own_sem.at[phase]).start()

        def one(k, carry):
            offset = n - 1 - k
            target = (me + offset) % n
            pltpu.make_async_remote_copy(
                src_ref=sky_block(phase, target),
                dst_ref=held.at[phase, me],
                send_sem=sky_send.at[phase],
                recv_sem=sky_recv.at[phase],
                device_id={"ell": target},
                device_id_type=pl.DeviceIdType.MESH,
            ).start()
            return carry

        lax.fori_loop(0, n - 1, one, 0)

    def others(phase, sem):
        block = held.at[phase, pl.ds(0, n - 1)]
        return pltpu.make_async_copy(block, block, sem.at[phase])

    def sum_copy(phase, level):
        size = n >> (level + 1)
        return pltpu.make_async_remote_copy(
            src_ref=part.at[phase, pl.ds(size, size)],
            dst_ref=got.at[phase, pl.ds(size - 1, size)],
            send_sem=sum_send.at[level, phase],
            recv_sem=sum_recv.at[level, phase],
            device_id={"ell": partner_of(level)},
            device_id_type=pl.DeviceIdType.MESH,
        )

    beam_copy = pltpu.make_async_copy(beam_ref.at[:, 0], beam_in.at[:, pl.ds(0, capacity)], beam_sem)
    beam_copy.start()

    barrier = pltpu.get_barrier_semaphore()

    def greet(k, carry):
        pl.semaphore_signal(
            barrier, inc=1, device_id={"ell": (me + 1 + k) % n}, device_id_type=pl.DeviceIdType.MESH
        )
        return carry

    lax.fori_loop(0, n - 1, greet, 0)
    pl.semaphore_wait(barrier, n - 1)

    for phase in range(min(LOOKAHEAD, phases)):
        send_sky(phase)

    for channel in range(channels):
        beam_in[channel, capacity] = jnp.zeros((components, depth), beam_in.dtype)
    local_rows = place.shape[1] // n

    def fill_place(quarter, carry):
        source = lax.broadcasted_iota(jnp.int32, (width, place.shape[1]), 0)
        column = lax.broadcasted_iota(jnp.int32, (width, place.shape[1]), 1)
        goal = (source // rows) * local_rows + source % rows + quarter * rows
        start = pl.multiple_of(quarter * width, width)
        place[pl.ds(start, width), :] = jnp.where(goal == column, 1.0, 0.0).astype(place.dtype)
        return carry

    lax.fori_loop(0, quarters, fill_place, 0)
    beam_copy.wait()

    def fill_dense(position, carry):
        base = dest_of(position) * BL_OWN
        for i in range(BL_OWN):
            slot = slot_ref[base + i]
            for channel in range(channels):
                dense[channel, position, i * components:(i + 1) * components, :] = beam_in[channel, slot]
        return carry

    lax.fori_loop(0, n, fill_dense, 0)

    def multiply(phase, first, count):
        channel = phase // quarters
        tile = dense.shape[2]

        def one(g, carry):
            at = first + g * GROUP
            left = dense[channel, pl.ds(at, GROUP)].reshape(GROUP * tile, depth)
            right = held[phase].reshape(width, depth)
            product = lax.dot_general(
                left, right, (((1,), (1,)), ((), ())), preferred_element_type=jnp.float32
            )
            part[phase, pl.ds(at, GROUP)] = product.reshape(GROUP, tile, width).astype(part.dtype)
            return carry

        lax.fori_loop(0, count // GROUP, one, 0)

    def add_level(phase, level):
        size = n >> (level + 1)
        sum_copy(phase, level).wait_recv()

        def one(q, carry):
            total = part[phase, q].astype(jnp.float32) + got[phase, q + size - 1].astype(jnp.float32)
            part[phase, q] = total.astype(part.dtype)
            return carry

        lax.fori_loop(0, size, one, 0)
        if level + 1 < levels:
            sum_copy(phase, level + 1).start()

    def step(t, carry):
        @pl.when(t + LOOKAHEAD < phases)
        def _():
            send_sky(t + LOOKAHEAD)

        for level in reversed(range(levels)):
            phase = t - 1 - level

            @pl.when((phase >= 0) & (phase < phases))
            def _():
                add_level(phase, level)

        @pl.when(t < phases)
        def _():
            pltpu.make_async_copy(sky_block(t, me), held.at[t, me], own_sem.at[t]).wait()
            others(t, sky_recv).wait()
            multiply(t, n // 2, n // 2)
            sum_copy(t, 0).start()
            multiply(t, 0, n // 2)

        return carry

    lax.fori_loop(0, phases + levels, step, 0)

    for channel in range(channels):
        total = jnp.zeros(out_ref.shape[1:], jnp.float32)
        for quarter in range(quarters):
            total = total + jnp.dot(
                part[channel * quarters + quarter, 0],
                place[quarter * width:(quarter + 1) * width, :],
                preferred_element_type=jnp.float32,
            )
        out_ref[channel] = total.astype(out_ref.dtype)

    def drain(phase, carry):
        others(phase, sky_send).wait()
        for level in range(levels):
            sum_copy(phase, level).wait_send()
        return carry

    lax.fori_loop(0, phases, drain, 0)


def local(n, sky_alm, beam_transfer, slot_rows, block_count):
    channels, local_rows = sky_alm.shape[:2]
    capacity, components, depth = beam_transfer.shape[2:]
    levels = n.bit_length() - 1
    quarters = local_rows // STEP_ROWS
    phases = channels * quarters
    width = n * STEP_ROWS
    tile = BL_OWN * components
    total_rows = BL_OWN * n
    slots = jnp.arange(capacity, dtype=jnp.int32)
    hit = (slot_rows[0][None, :] == jnp.arange(total_rows, dtype=jnp.int32)[:, None]) & (slots < block_count[0])[None, :]
    slot_of_row = jnp.min(jnp.where(hit, slots[None, :], capacity), axis=1)
    out = pl.pallas_call(
        functools.partial(kernel, n, levels, quarters),
        out_shape=jax.ShapeDtypeStruct((channels, tile, n * local_rows), jnp.bfloat16),
        in_specs=[
            pl.BlockSpec(memory_space=pltpu.SMEM),
            pl.BlockSpec(memory_space=pl.ANY),
            pl.BlockSpec(memory_space=pl.ANY),
        ],
        out_specs=pl.BlockSpec(memory_space=pltpu.VMEM),
        scratch_shapes=[
            pltpu.VMEM((channels, capacity + 1, components, depth), jnp.bfloat16),
            pltpu.VMEM((channels, n, tile, depth), jnp.bfloat16),
            pltpu.VMEM((phases, n, STEP_ROWS, depth), jnp.bfloat16),
            pltpu.VMEM((phases, n, tile, width), jnp.bfloat16),
            pltpu.VMEM((phases, n - 1, tile, width), jnp.bfloat16),
            pltpu.VMEM((quarters * width, n * local_rows), jnp.bfloat16),
            pltpu.SemaphoreType.DMA,
            pltpu.SemaphoreType.DMA((phases,)),
            pltpu.SemaphoreType.DMA((phases,)),
            pltpu.SemaphoreType.DMA((phases,)),
            pltpu.SemaphoreType.DMA((levels, phases)),
            pltpu.SemaphoreType.DMA((levels, phases)),
        ],
        compiler_params=pltpu.CompilerParams(
            collective_id=0, has_side_effects=True, vmem_limit_bytes=67043328
        ),
    )(slot_of_row, sky_alm, beam_transfer)
    return out.reshape(channels, BL_OWN, components, n * local_rows)


def solution(mesh):
    in_specs = (
        P("chan", "ell", None),
        P("chan", "ell", None, None, None),
        P("ell", None),
        P("ell"),
    )
    out_specs = P("chan", "ell", None, None)
    return jax.shard_map(
        functools.partial(local, mesh.shape["ell"]),
        mesh=mesh,
        in_specs=in_specs,
        out_specs=out_specs,
        check_vma=False,
    )
```

```python
import functools

import jax
import jax.numpy as jnp
from jax import lax
from jax.experimental import pallas as pl
from jax.experimental.pallas import tpu as pltpu
from jax.sharding import PartitionSpec as P

BL_OWN = 8
LOOKAHEAD = 1
STEP_ROWS = 16
GROUP = 4


def bit(value, at):
    return (value // (1 << at)) % 2


def kernel(n, levels, quarters, rows_ref, count_ref, sky_ref, beam_ref, out_ref, slot_vec, slot_ref, beam_in, dense, held, part, got, place,
           slot_sem, beam_sem, own_sem, sky_send, sky_recv, sum_send, sum_recv):
    me = lax.axis_index("ell")
    channels, capacity, components = beam_in.shape[0], beam_in.shape[1] - 1, beam_in.shape[2]
    depth = beam_in.shape[3]
    phases = channels * quarters
    release = phases - 2
    rows = STEP_ROWS
    width = n * rows

    def dest_of(position):
        total = 0
        for level in range(levels):
            flip = bit(position, levels - 1 - level)
            total = total + ((bit(me, level) + flip) % 2) * (1 << level)
        return total

    def partner_of(level):
        return me + (1 - 2 * bit(me, level)) * (1 << level)

    def sky_block(phase, owner):
        channel, quarter = phase // quarters, phase % quarters
        return sky_ref.at[
            channel,
            pl.ds(pl.multiple_of(quarter * rows, rows), rows),
            pl.ds(pl.multiple_of(owner * depth, 128), depth),
        ]

    def send_sky(phase):
        pltpu.make_async_copy(sky_block(phase, me), held.at[phase, me], own_sem.at[phase]).start()

        def one(k, carry):
            target = (me + n - 1 - k) % n
            pltpu.make_async_remote_copy(
                src_ref=sky_block(phase, target),
                dst_ref=held.at[phase, me],
                send_sem=sky_send.at[phase],
                recv_sem=sky_recv.at[phase],
                device_id={"ell": target},
                device_id_type=pl.DeviceIdType.MESH,
            ).start()
            return carry

        lax.fori_loop(0, n - 1, one, 0)

    def others(phase, sem):
        block = held.at[phase, pl.ds(0, n - 1)]
        return pltpu.make_async_copy(block, block, sem.at[phase])

    def sum_copy(phase, level):
        size = n >> (level + 1)
        return pltpu.make_async_remote_copy(
            src_ref=part.at[phase, pl.ds(size, size)],
            dst_ref=got.at[phase, pl.ds(size - 1, size)],
            send_sem=sum_send.at[level, phase],
            recv_sem=sum_recv.at[level, phase],
            device_id={"ell": partner_of(level)},
            device_id_type=pl.DeviceIdType.MESH,
        )

    beam_copy = pltpu.make_async_copy(beam_ref.at[:, 0], beam_in.at[:, pl.ds(0, capacity)], beam_sem)
    beam_copy.start()

    barrier = pltpu.get_barrier_semaphore()

    def greet(k, carry):
        pl.semaphore_signal(
            barrier, inc=1, device_id={"ell": (me + 1 + k) % n}, device_id_type=pl.DeviceIdType.MESH
        )
        return carry

    lax.fori_loop(0, n - 1, greet, 0)
    pl.semaphore_wait(barrier, n - 1)

    for phase in range(min(LOOKAHEAD, phases)):
        send_sky(phase)

    shape = (capacity, n * BL_OWN)
    slots = lax.broadcasted_iota(jnp.int32, shape, 0)
    held_rows = jnp.broadcast_to(rows_ref[...], shape[::-1]).T
    hit = (held_rows == lax.broadcasted_iota(jnp.int32, shape, 1)) & (slots < count_ref[0])
    slot_vec[...] = jnp.min(jnp.where(hit, slots, capacity), axis=0, keepdims=True)
    slot_copy = pltpu.make_async_copy(slot_vec, slot_ref, slot_sem)
    slot_copy.start()

    for channel in range(channels):
        beam_in[channel, capacity] = jnp.zeros((components, depth), beam_in.dtype)
    local_rows = place.shape[1] // n

    def fill_place(quarter, carry):
        source = lax.broadcasted_iota(jnp.int32, (width, place.shape[1]), 0)
        column = lax.broadcasted_iota(jnp.int32, (width, place.shape[1]), 1)
        goal = (source // rows) * local_rows + source % rows + quarter * rows
        start = pl.multiple_of(quarter * width, width)
        place[pl.ds(start, width), :] = jnp.where(goal == column, 1.0, 0.0).astype(place.dtype)
        return carry

    lax.fori_loop(0, quarters, fill_place, 0)
    slot_copy.wait()
    beam_copy.wait()

    def fill_dense(position, carry):
        base = dest_of(position) * BL_OWN
        for i in range(BL_OWN):
            slot = slot_ref[0, base + i]
            for channel in range(channels):
                dense[channel, position, i * components:(i + 1) * components, :] = beam_in[channel, slot]
        return carry

    lax.fori_loop(0, n, fill_dense, 0)

    def multiply(phase, first, count):
        channel = phase // quarters
        tile = dense.shape[2]

        def one(g, carry):
            at = first + g * GROUP
            left = dense[channel, pl.ds(at, GROUP)].reshape(GROUP * tile, depth)
            right = held[phase].reshape(width, depth)
            product = lax.dot_general(
                left, right, (((1,), (1,)), ((), ())), preferred_element_type=jnp.float32
            )
            part[phase, pl.ds(at, GROUP)] = product.reshape(GROUP, tile, width).astype(part.dtype)
            return carry

        lax.fori_loop(0, count // GROUP, one, 0)

    def add_level(phase, level, send):
        size = n >> (level + 1)
        sum_copy(phase, level).wait_recv()

        def one(q, carry):
            total = part[phase, q].astype(jnp.float32) + got[phase, q + size - 1].astype(jnp.float32)
            part[phase, q] = total.astype(part.dtype)
            return carry

        lax.fori_loop(0, size, one, 0)

        @pl.when(send)
        def _():
            sum_copy(phase, min(level + 1, levels - 1)).start()

    def step(t, carry):
        @pl.when(t + LOOKAHEAD < phases)
        def _():
            send_sky(t + LOOKAHEAD)

        for level in range(levels - 1):
            phase = t - 1 - level

            @pl.when((phase >= 0) & (phase < phases))
            def _():
                add_level(phase, level, t >= release if level == levels - 2 else t >= 0)

        @pl.when(t == release)
        def _():
            def one(phase, inner):
                sum_copy(phase, levels - 1).start()
                return inner

            lax.fori_loop(0, release - levels + 1, one, 0)

        @pl.when(t < phases)
        def _():
            pltpu.make_async_copy(sky_block(t, me), held.at[t, me], own_sem.at[t]).wait()
            others(t, sky_recv).wait()
            multiply(t, n // 2, n // 2)
            sum_copy(t, 0).start()
            multiply(t, 0, n // 2)

        return carry

    lax.fori_loop(0, phases + levels - 1, step, 0)

    def finish(phase, carry):
        add_level(phase, levels - 1, phase < 0)
        return carry

    lax.fori_loop(0, phases, finish, 0)

    for channel in range(channels):
        total = jnp.zeros(out_ref.shape[1:], jnp.float32)
        for quarter in range(quarters):
            total = total + jnp.dot(
                part[channel * quarters + quarter, 0],
                place[quarter * width:(quarter + 1) * width, :],
                preferred_element_type=jnp.float32,
            )
        out_ref[channel] = total.astype(out_ref.dtype)

    def drain(phase, carry):
        others(phase, sky_send).wait()
        for level in range(levels):
            sum_copy(phase, level).wait_send()
        return carry

    lax.fori_loop(0, phases, drain, 0)


def local(n, sky_alm, beam_transfer, slot_rows, block_count):
    channels, local_rows = sky_alm.shape[:2]
    capacity, components, depth = beam_transfer.shape[2:]
    levels = n.bit_length() - 1
    quarters = local_rows // STEP_ROWS
    phases = channels * quarters
    width = n * STEP_ROWS
    tile = BL_OWN * components
    out = pl.pallas_call(
        functools.partial(kernel, n, levels, quarters),
        out_shape=jax.ShapeDtypeStruct((channels, tile, n * local_rows), jnp.bfloat16),
        in_specs=[
            pl.BlockSpec(memory_space=pltpu.VMEM),
            pl.BlockSpec(memory_space=pltpu.SMEM),
            pl.BlockSpec(memory_space=pl.ANY),
            pl.BlockSpec(memory_space=pl.ANY),
        ],
        out_specs=pl.BlockSpec(memory_space=pltpu.VMEM),
        scratch_shapes=[
            pltpu.VMEM((1, n * BL_OWN), jnp.int32),
            pltpu.SMEM((1, n * BL_OWN), jnp.int32),
            pltpu.VMEM((channels, capacity + 1, components, depth), jnp.bfloat16),
            pltpu.VMEM((channels, n, tile, depth), jnp.bfloat16),
            pltpu.VMEM((phases, n, STEP_ROWS, depth), jnp.bfloat16),
            pltpu.VMEM((phases, n, tile, width), jnp.bfloat16),
            pltpu.VMEM((phases, n - 1, tile, width), jnp.bfloat16),
            pltpu.VMEM((quarters * width, n * local_rows), jnp.bfloat16),
            pltpu.SemaphoreType.DMA,
            pltpu.SemaphoreType.DMA,
            pltpu.SemaphoreType.DMA((phases,)),
            pltpu.SemaphoreType.DMA((phases,)),
            pltpu.SemaphoreType.DMA((phases,)),
            pltpu.SemaphoreType.DMA((levels, phases)),
            pltpu.SemaphoreType.DMA((levels, phases)),
        ],
        compiler_params=pltpu.CompilerParams(
            collective_id=0, has_side_effects=True, vmem_limit_bytes=67043328
        ),
    )(slot_rows, block_count, sky_alm, beam_transfer)
    return out.reshape(channels, BL_OWN, components, n * local_rows)


def solution(mesh):
    in_specs = (
        P("chan", "ell", None),
        P("chan", "ell", None, None, None),
        P("ell", None),
        P("ell"),
    )
    out_specs = P("chan", "ell", None, None)
    return jax.shard_map(
        functools.partial(local, mesh.shape["ell"]),
        mesh=mesh,
        in_specs=in_specs,
        out_specs=out_specs,
        check_vma=False,
    )
```

```python
import functools

import jax
import jax.numpy as jnp
from jax import lax
from jax.experimental import pallas as pl
from jax.experimental.pallas import tpu as pltpu
from jax.sharding import PartitionSpec as P

BL_OWN = 8
LOOKAHEAD = 1
STEP_ROWS = 16
GROUP = 4


def bit(value, at):
    return (value // (1 << at)) % 2


def kernel(n, levels, quarters, rows_ref, count_ref, sky_ref, beam_ref, out_ref, slot_vec, slot_ref, beam_in, dense, held, part, got, place, gathered,
           slot_sem, beam_sem, own_sem, sky_send, sky_recv, sum_send, sum_recv):
    me = lax.axis_index("ell")
    channels, capacity, components = beam_in.shape[0], beam_in.shape[1] - 1, beam_in.shape[2]
    depth = beam_in.shape[3]
    phases = channels * quarters
    release = phases - 2
    rows = STEP_ROWS
    width = n * rows

    def dest_of(position):
        total = 0
        for level in range(levels):
            flip = bit(position, levels - 1 - level)
            total = total + ((bit(me, level) + flip) % 2) * (1 << level)
        return total

    def partner_of(level):
        return me + (1 - 2 * bit(me, level)) * (1 << level)

    def sky_block(phase, owner):
        channel, quarter = phase // quarters, phase % quarters
        return sky_ref.at[
            channel,
            pl.ds(pl.multiple_of(quarter * rows, rows), rows),
            pl.ds(pl.multiple_of(owner * depth, 128), depth),
        ]

    def send_sky(phase):
        pltpu.make_async_copy(sky_block(phase, me), held.at[phase, me], own_sem.at[phase]).start()

        def one(k, carry):
            target = (me + n - 1 - k) % n
            pltpu.make_async_remote_copy(
                src_ref=sky_block(phase, target),
                dst_ref=held.at[phase, me],
                send_sem=sky_send.at[phase],
                recv_sem=sky_recv.at[phase],
                device_id={"ell": target},
                device_id_type=pl.DeviceIdType.MESH,
            ).start()
            return carry

        lax.fori_loop(0, n - 1, one, 0)

    def others(phase, sem):
        block = held.at[phase, pl.ds(0, n - 1)]
        return pltpu.make_async_copy(block, block, sem.at[phase])

    def sum_copy(phase, level):
        size = n >> (level + 1)
        return pltpu.make_async_remote_copy(
            src_ref=part.at[phase, pl.ds(size, size)],
            dst_ref=got.at[phase, pl.ds(size - 1, size)],
            send_sem=sum_send.at[level, phase],
            recv_sem=sum_recv.at[level, phase],
            device_id={"ell": partner_of(level)},
            device_id_type=pl.DeviceIdType.MESH,
        )

    beam_copy = pltpu.make_async_copy(beam_ref.at[:, 0], beam_in.at[:, pl.ds(0, capacity)], beam_sem)
    beam_copy.start()

    barrier = pltpu.get_barrier_semaphore()

    def greet(k, carry):
        pl.semaphore_signal(
            barrier, inc=1, device_id={"ell": (me + 1 + k) % n}, device_id_type=pl.DeviceIdType.MESH
        )
        return carry

    lax.fori_loop(0, n - 1, greet, 0)
    pl.semaphore_wait(barrier, n - 1)

    for phase in range(min(LOOKAHEAD, phases)):
        send_sky(phase)

    shape = (capacity, n * BL_OWN)
    slots = lax.broadcasted_iota(jnp.int32, shape, 0)
    held_rows = jnp.broadcast_to(rows_ref[...], shape[::-1]).T
    hit = (held_rows == lax.broadcasted_iota(jnp.int32, shape, 1)) & (slots < count_ref[0])
    slot_vec[...] = jnp.min(jnp.where(hit, slots, capacity), axis=0, keepdims=True)
    slot_copy = pltpu.make_async_copy(slot_vec, slot_ref, slot_sem)
    slot_copy.start()

    for channel in range(channels):
        beam_in[channel, capacity] = jnp.zeros((components, depth), beam_in.dtype)
    local_rows = place.shape[1] // n

    def fill_place(quarter, carry):
        source = lax.broadcasted_iota(jnp.int32, (width, place.shape[1]), 0)
        column = lax.broadcasted_iota(jnp.int32, (width, place.shape[1]), 1)
        goal = (source // rows) * local_rows + source % rows + quarter * rows
        start = pl.multiple_of(quarter * width, width)
        place[pl.ds(start, width), :] = jnp.where(goal == column, 1.0, 0.0).astype(place.dtype)
        return carry

    lax.fori_loop(0, quarters, fill_place, 0)
    slot_copy.wait()
    beam_copy.wait()

    def fill_dense(position, carry):
        base = dest_of(position) * BL_OWN
        for i in range(BL_OWN):
            slot = slot_ref[0, base + i]
            for channel in range(channels):
                dense[channel, position, i * components:(i + 1) * components, :] = beam_in[channel, slot]
        return carry

    lax.fori_loop(0, n, fill_dense, 0)

    def multiply(phase, first, count):
        channel = phase // quarters
        tile = dense.shape[2]

        def one(g, carry):
            at = first + g * GROUP
            left = dense[channel, pl.ds(at, GROUP)].reshape(GROUP * tile, depth)
            right = held[phase].reshape(width, depth)
            product = lax.dot_general(
                left, right, (((1,), (1,)), ((), ())), preferred_element_type=jnp.float32
            )
            part[phase, pl.ds(at, GROUP)] = product.reshape(GROUP, tile, width).astype(part.dtype)
            return carry

        lax.fori_loop(0, count // GROUP, one, 0)

    def add_level(phase, level, send):
        size = n >> (level + 1)
        sum_copy(phase, level).wait_recv()

        def one(q, carry):
            total = part[phase, q].astype(jnp.float32) + got[phase, q + size - 1].astype(jnp.float32)
            part[phase, q] = total.astype(part.dtype)
            return carry

        lax.fori_loop(0, size, one, 0)

        @pl.when(send)
        def _():
            sum_copy(phase, min(level + 1, levels - 1)).start()

    def step(t, carry):
        @pl.when(t + LOOKAHEAD < phases)
        def _():
            send_sky(t + LOOKAHEAD)

        for level in range(levels - 1):
            phase = t - 1 - level

            @pl.when((phase >= 0) & (phase < phases))
            def _():
                add_level(phase, level, t >= release if level == levels - 2 else t >= 0)

        @pl.when(t == release)
        def _():
            def one(phase, inner):
                sum_copy(phase, levels - 1).start()
                return inner

            lax.fori_loop(0, release - levels + 1, one, 0)

        @pl.when(t < phases)
        def _():
            pltpu.make_async_copy(sky_block(t, me), held.at[t, me], own_sem.at[t]).wait()
            others(t, sky_recv).wait()
            multiply(t, n // 2, n // 2)
            sum_copy(t, 0).start()
            multiply(t, 0, n // 2)

        return carry

    lax.fori_loop(0, phases + levels - 1, step, 0)

    def finish(phase, carry):
        add_level(phase, levels - 1, phase < 0)
        return carry

    def placed(phase):
        quarter = phase % quarters
        return jnp.dot(
            part[phase, 0], place[quarter * width:(quarter + 1) * width, :], preferred_element_type=jnp.float32
        )

    lax.fori_loop(0, phases - 1, finish, 0)
    for channel in range(channels):
        first = channel * quarters
        last = first + quarters
        total = jnp.zeros(out_ref.shape[1:], jnp.float32)
        for phase in range(first, min(last, phases - 1)):
            total = total + placed(phase)
        if last == phases:
            gathered[...] = total
        else:
            out_ref[channel] = total.astype(out_ref.dtype)
    finish(phases - 1, 0)
    out_ref[channels - 1] = (gathered[...] + placed(phases - 1)).astype(out_ref.dtype)

    def drain(phase, carry):
        others(phase, sky_send).wait()
        for level in range(levels):
            sum_copy(phase, level).wait_send()
        return carry

    lax.fori_loop(0, phases, drain, 0)


def local(n, sky_alm, beam_transfer, slot_rows, block_count):
    channels, local_rows = sky_alm.shape[:2]
    capacity, components, depth = beam_transfer.shape[2:]
    levels = n.bit_length() - 1
    quarters = local_rows // STEP_ROWS
    phases = channels * quarters
    width = n * STEP_ROWS
    tile = BL_OWN * components
    out = pl.pallas_call(
        functools.partial(kernel, n, levels, quarters),
        out_shape=jax.ShapeDtypeStruct((channels, tile, n * local_rows), jnp.bfloat16),
        in_specs=[
            pl.BlockSpec(memory_space=pltpu.VMEM),
            pl.BlockSpec(memory_space=pltpu.SMEM),
            pl.BlockSpec(memory_space=pl.ANY),
            pl.BlockSpec(memory_space=pl.ANY),
        ],
        out_specs=pl.BlockSpec(memory_space=pltpu.VMEM),
        scratch_shapes=[
            pltpu.VMEM((1, n * BL_OWN), jnp.int32),
            pltpu.SMEM((1, n * BL_OWN), jnp.int32),
            pltpu.VMEM((channels, capacity + 1, components, depth), jnp.bfloat16),
            pltpu.VMEM((channels, n, tile, depth), jnp.bfloat16),
            pltpu.VMEM((phases, n, STEP_ROWS, depth), jnp.bfloat16),
            pltpu.VMEM((phases, n, tile, width), jnp.bfloat16),
            pltpu.VMEM((phases, n - 1, tile, width), jnp.bfloat16),
            pltpu.VMEM((quarters * width, n * local_rows), jnp.bfloat16),
            pltpu.VMEM((tile, n * local_rows), jnp.float32),
            pltpu.SemaphoreType.DMA,
            pltpu.SemaphoreType.DMA,
            pltpu.SemaphoreType.DMA((phases,)),
            pltpu.SemaphoreType.DMA((phases,)),
            pltpu.SemaphoreType.DMA((phases,)),
            pltpu.SemaphoreType.DMA((levels, phases)),
            pltpu.SemaphoreType.DMA((levels, phases)),
        ],
        compiler_params=pltpu.CompilerParams(
            collective_id=0, has_side_effects=True, vmem_limit_bytes=67043328
        ),
    )(slot_rows, block_count, sky_alm, beam_transfer)
    return out.reshape(channels, BL_OWN, components, n * local_rows)


def solution(mesh):
    in_specs = (
        P("chan", "ell", None),
        P("chan", "ell", None, None, None),
        P("ell", None),
        P("ell"),
    )
    out_specs = P("chan", "ell", None, None)
    return jax.shard_map(
        functools.partial(local, mesh.shape["ell"]),
        mesh=mesh,
        in_specs=in_specs,
        out_specs=out_specs,
        check_vma=False,
    )
```
